32 devices in a mesh: dp: 8 (over z, y), tensor: 4 (over x, core).
Axes of the slice: x: 2, y: 2, z: 4, core: 2. Of those that a mesh axis runs over, the one named last changes fastest.
Arguments:
- block_input: bfloat16 [8192, 1536], P(('dp', 'tensor')), may hold values from -6 to 6
- segment_ids: int32 [8, 1024], P('dp'), may hold values from 0 to 3, as said below
- gain_attn: float32 [1536], replicated, may hold values from 0.5 to 1.5
- w_query: bfloat16 [1536, 1536], P('dp', 'tensor'), may hold values from -0.15625 to 0.15625
- b_query: float32 [1536], P('tensor'), may hold values from -3 to 3
- w_keyval: bfloat16 [1536, 512], P('dp'), may hold values from -0.15625 to 0.15625
- b_keyval: float32 [512], replicated, may hold values from -3 to 3
- w_out: bfloat16 [1536, 1536], P('tensor', 'dp'), may hold values from -0.625 to 0.625
- gain_ffn: float32 [1536], replicated, may hold values from 0.5 to 1.5
- w_gate: bfloat16 [1536, 8960], P('dp', 'tensor'), may hold values from -0.15625 to 0.15625
- w_up: bfloat16 [1536, 8960], P('dp', 'tensor'), may hold values from -0.15625 to 0.15625
- w_down: bfloat16 [8960, 1536], P('tensor', 'dp'), may hold values from -0.0625 to 0.0625
- cotangent: bfloat16 [8192, 1536], P(('dp', 'tensor')), may hold values from -6 to 6
Outputs:
- block_output: bfloat16 [8192, 1536], P(('dp', 'tensor'))
- grad_input: bfloat16 [8192, 1536], P(('dp', 'tensor'))
- grad_gain_attn: float32 [1536], P(('dp', 'tensor'))
- grad_w_query: float32 [1536, 1536], P('dp', 'tensor')
- grad_b_query: float32 [1536], P(('dp', 'tensor'))
- grad_w_keyval: float32 [1536, 512], P(('dp', 'tensor'))
- grad_b_keyval: float32 [512], P(('dp', 'tensor'))
- grad_w_out: float32 [1536, 1536], P('tensor', 'dp')
- grad_gain_ffn: float32 [1536], P(('dp', 'tensor'))
- grad_w_gate: float32 [1536, 8960], P('dp', 'tensor')
- grad_w_up: float32 [1536, 8960], P('dp', 'tensor')
- grad_w_down: float32 [8960, 1536], P('tensor', 'dp')
The draws below stay inside these ranges and needn't reach their ends.
Inputs may be any that keep to these rules, and one draw needn't show every extreme that they name: `segment_ids`: ids start at 0 and never fall along a sequence, each rising by one at a document's start; a sequence holds 2 to 4 documents, each of 204 tokens or more; some sequence holds 4.
All inputs are finite; a program needn't handle non-finite values.
Results may differ from the reference program's by a relative error of at most 0.018.
Values may be sent and summed in bfloat16 or wider, within the bound.
No kernel may reach another device: no remote copies, remote signals or barrier semaphores. Data moves between devices by JAX's collectives and lax.ppermute only.
A program may use at most 256 MiB of HBM per device.

```python
import math
import jax
import jax.numpy as jnp
from jax import lax

D = 1536
HQ = 12
KV = 2
HD = 128
FF = 8960
SEQ_LEN = 1024
SEQS = 8
TOKENS = 8192
N_TENSOR = 4


def draw_segment_ids(key, part):
    least = SEQ_LEN // 5
    doc_count = jax.random.randint(jax.random.fold_in(key, 21), (SEQS,), 2, 5)
    doc_count = doc_count.at[0].set(4)
    spare = SEQ_LEN - doc_count * least
    cuts = jax.random.randint(jax.random.fold_in(key, 22), (SEQS, 3), 0, SEQ_LEN)
    cuts = cuts % (spare[:, None] + 1)
    slot = jnp.arange(3, dtype=jnp.int32)
    cuts = jnp.where(slot[None, :] < doc_count[:, None] - 1, cuts, spare[:, None])
    cuts = jnp.sort(cuts, axis=1)
    bounds = (slot[None, :] + 1) * least + cuts
    index_row = jnp.arange(SEQ_LEN, dtype=jnp.int32)
    passed = (index_row[None, :, None] >= bounds[:, None, :]).astype(jnp.int32)
    return jnp.sum(passed, axis=2).astype(jnp.int32)


def level_of(stream_key, dims, split, low, largest):
    def one(axis_at, parts):
        steps = jax.random.uniform(jax.random.fold_in(jax.random.fold_in(stream_key, 6), axis_at), (parts,), jnp.float32, low / len(split), largest / len(split))
        return jnp.repeat(jnp.exp(steps), dims[axis_at] // parts).reshape((-1,) + (1,) * (len(dims) - axis_at - 1))

    level = one(*split[0])
    for cut in split[1:]:
        level = level * one(*cut)
    return level


def bell_draw(rng, dims, deviation, limit, shards=(), held_as=jnp.bfloat16):
    level = level_of(rng, dims, shards, -0.22, 0.18) if shards else 1.0
    result = jax.random.normal(rng, dims, jnp.float32) * deviation * level
    return jnp.minimum(jnp.maximum(result, -limit), limit).astype(held_as)


def setup_inputs(seed: int = 0) -> dict:
    key_of = jax.random.split(jax.random.key(seed), 14)
    block_input = bell_draw(key_of[0], (TOKENS, D), 1.0, 6.0, ((0, 32),))
    segment_ids = draw_segment_ids(jax.random.fold_in(key_of[13], 71), 0)
    gain_attn = jnp.clip(1.0 + 0.1 * jax.random.normal(key_of[2], (D,), jnp.float32), 0.5, 1.5)
    w_query = bell_draw(key_of[3], (D, HQ * HD), D ** -0.5, 0.15625, ((0, 8), (1, 4)))
    b_query = bell_draw(key_of[4], (HQ * HD,), 0.5, 3.0, ((0, 4),), jnp.float32)
    w_keyval = bell_draw(key_of[5], (D, 2 * KV * HD), D ** -0.5, 0.15625, ((0, 8),))
    b_keyval = bell_draw(key_of[6], (2 * KV * HD,), 0.5, 3.0, (), jnp.float32)
    w_out = bell_draw(key_of[7], (HQ * HD, D), (HQ * HD // 16) ** -0.5, 0.625, ((0, 4), (1, 8)))
    gain_ffn = jnp.clip(1.0 + 0.1 * jax.random.normal(key_of[8], (D,), jnp.float32), 0.5, 1.5)
    w_gate = bell_draw(key_of[9], (D, FF), D ** -0.5, 0.15625, ((0, 8), (1, 4)))
    w_up = bell_draw(key_of[10], (D, FF), D ** -0.5, 0.15625, ((0, 8), (1, 4)))
    w_down = bell_draw(key_of[11], (FF, D), FF ** -0.5, 0.0625, ((0, 4), (1, 8)))
    cotangent = bell_draw(key_of[12], (TOKENS, D), 1.0, 6.0, ((0, 32),))
    return {"block_input": block_input, "segment_ids": segment_ids, "gain_attn": gain_attn, "w_query": w_query, "b_query": b_query, "w_keyval": w_keyval, "b_keyval": b_keyval, "w_out": w_out, "gain_ffn": gain_ffn, "w_gate": w_gate, "w_up": w_up, "w_down": w_down, "cotangent": cotangent}


epsilon = 1e-06
rope_base = 1000000.0
masked_score = -1e+30

def matmul(left, right):
    return jnp.dot(left, right, preferred_element_type=jnp.float32)

def lowered(values_in):
    return lax.optimization_barrier(values_in.astype(jnp.bfloat16))

def positions_of(segment_row):
    index_row = jnp.arange(segment_row.shape[0], dtype=jnp.int32)
    starts = jnp.concatenate([jnp.ones((1,), jnp.int32), (segment_row[1:] != segment_row[:-1]).astype(jnp.int32)])
    first_index = lax.cummax(jnp.where(starts > 0, index_row, 0), axis=0)
    return index_row - first_index

def allowed_of(segment_row):
    index_row = jnp.arange(segment_row.shape[0], dtype=jnp.int32)
    causal = index_row[:, None] >= index_row[None, :]
    return causal & (segment_row[:, None] == segment_row[None, :])

def rotary(positions):
    inverse = rope_base ** (-(jnp.arange(HD // 2, dtype=jnp.float32) * 2.0 / HD))
    angles = positions.astype(jnp.float32)[:, None] * inverse[None, :]
    angles = jnp.concatenate([angles, angles], axis=1)
    return (jnp.cos(angles), jnp.sin(angles))

def turn(values_in, cosine_table, sine_table):
    half_size = values_in.shape[-1] // 2
    rolled = jnp.concatenate([-values_in[..., half_size:], values_in[..., :half_size]], axis=-1)
    return values_in * cosine_table + rolled * sine_table

def norm_forward(values_in):
    row_scale = lax.rsqrt(lax.optimization_barrier(jnp.mean(values_in * values_in, axis=-1, keepdims=True)) + epsilon)
    return (values_in * row_scale, row_scale)

def norm_backward(grad_out, normed, row_scale, gain_vec):
    grad_normed = grad_out * gain_vec
    grad_in = row_scale * (grad_normed - normed * lax.optimization_barrier(jnp.mean(grad_normed * normed, axis=-1, keepdims=True)))
    return (grad_in, lax.optimization_barrier(jnp.sum(grad_out * normed, axis=0)))

def reference(block_input, segment_ids, gain_attn, w_query, b_query, w_keyval, b_keyval, w_out, gain_ffn, w_gate, w_up, w_down, cotangent):
    seq_count = segment_ids.shape[0]
    seq_length = segment_ids.shape[1]
    heads_dev = HQ // N_TENSOR
    group_size = HQ // KV
    kv_of = jnp.arange(HQ, dtype=jnp.int32) // group_size
    root_size = math.sqrt(HD)
    inputs_seq = block_input.reshape(seq_count, seq_length, D)
    cot_seq = cotangent.reshape(seq_count, seq_length, D)

    def one_sequence(totals, seq_items):
        rows_in, segment_row, rows_cot = seq_items
        rows_float = rows_in.astype(jnp.float32)
        normed_one, scale_one = norm_forward(rows_float)
        act_one = lowered(normed_one * gain_attn)
        query_rows = matmul(act_one, w_query) + b_query
        keyval = matmul(act_one, w_keyval) + b_keyval
        cosine_table, sine_table = rotary(positions_of(segment_row))
        cos_heads = cosine_table[:, None, :]
        sin_heads = sine_table[:, None, :]
        query_rot = lowered(turn(query_rows.reshape(seq_length, HQ, HD), cos_heads, sin_heads)).astype(jnp.float32)
        key_rot = lowered(turn(keyval[:, :KV * HD].reshape(seq_length, KV, HD), cos_heads, sin_heads)).astype(jnp.float32)
        value_rows = lowered(keyval[:, KV * HD:].reshape(seq_length, KV, HD)).astype(jnp.float32)
        key_heads = key_rot[:, kv_of]
        value_heads = value_rows[:, kv_of]
        allowed = allowed_of(segment_row)
        raw_scores = jnp.einsum('qhd,khd->hqk', query_rot, key_heads) / root_size
        scores = jnp.where(allowed[None], raw_scores, masked_score)
        row_max = lax.optimization_barrier(jnp.max(scores, axis=2, keepdims=True))
        log_total = row_max + jnp.log(lax.optimization_barrier(jnp.sum(jnp.exp(scores - row_max), axis=2, keepdims=True)))
        attn_probs = jnp.exp(scores - log_total)
        probs_low = lowered(attn_probs).astype(jnp.float32)
        attn_result = jnp.einsum('hqk,khd->qhd', probs_low, value_heads)
        context = lowered(attn_result.reshape(seq_length, HQ * HD))
        hidden = rows_float + matmul(context, w_out)
        normed_two, scale_two = norm_forward(hidden)
        act_two = lowered(normed_two * gain_ffn)
        gate_pre = matmul(act_two, w_gate)
        up_part = matmul(act_two, w_up)
        sigmoid_gate = jax.nn.sigmoid(gate_pre)
        silu_gate = gate_pre * sigmoid_gate
        mixed_rows = lowered(silu_gate * up_part)
        block_out = (hidden + matmul(mixed_rows, w_down)).astype(jnp.bfloat16)
        grad_mixed = matmul(rows_cot, w_down.T)
        grad_gate = lowered(grad_mixed * up_part * sigmoid_gate * (1.0 + gate_pre * (1.0 - sigmoid_gate)))
        grad_up = lowered(grad_mixed * silu_gate)
        grad_act_two = matmul(grad_gate, w_gate.T) + matmul(grad_up, w_up.T)
        back_two, gain_two = norm_backward(grad_act_two, normed_two, scale_two, gain_ffn)
        grad_hidden = rows_cot.astype(jnp.float32) + back_two
        grad_attn = lowered(grad_hidden)
        grad_context = lowered(matmul(grad_attn, w_out.T)).astype(jnp.float32).reshape(seq_length, HQ, HD)
        grad_probs = jnp.einsum('qhd,khd->hqk', grad_context, value_heads)
        row_delta = lax.optimization_barrier(jnp.sum(grad_context * attn_result, axis=2)).T[:, :, None]
        grad_scores = lowered(attn_probs * (grad_probs - row_delta)).astype(jnp.float32)
        grad_query_rot = jnp.einsum('hqk,khd->qhd', grad_scores, key_heads) / root_size
        grad_key_heads = jnp.einsum('hqk,qhd->khd', grad_scores, query_rot) / root_size
        grad_value_heads = jnp.einsum('hqk,qhd->khd', probs_low, grad_context)
        grad_query = turn(grad_query_rot, cos_heads, -sin_heads).reshape(seq_length, HQ * HD)
        grad_key_dev = turn(grad_key_heads.reshape(seq_length, N_TENSOR, heads_dev, HD).sum(axis=2), cos_heads, -sin_heads)
        grad_value_dev = grad_value_heads.reshape(seq_length, N_TENSOR, heads_dev, HD).sum(axis=2)
        grad_query_low = lowered(grad_query)
        grad_act_one = matmul(grad_query_low, w_query.T)
        grad_wkv = jnp.zeros((D, 2 * KV * HD), jnp.float32)
        grad_bkv = jnp.zeros((2 * KV * HD,), jnp.float32)
        for tensor_slot in range(N_TENSOR):
            head_kv = tensor_slot * heads_dev // group_size
            key_col = head_kv * HD
            value_col = KV * HD + head_kv * HD
            key_low = lowered(grad_key_dev[:, tensor_slot])
            value_low = lowered(grad_value_dev[:, tensor_slot])
            grad_wkv = grad_wkv.at[:, key_col:key_col + HD].add(matmul(act_one.T, key_low))
            grad_wkv = grad_wkv.at[:, value_col:value_col + HD].add(matmul(act_one.T, value_low))
            grad_act_one = grad_act_one + matmul(key_low, w_keyval[:, key_col:key_col + HD].T)
            grad_act_one = grad_act_one + matmul(value_low, w_keyval[:, value_col:value_col + HD].T)
            grad_bkv = grad_bkv.at[key_col:key_col + HD].add(lax.optimization_barrier(jnp.sum(grad_key_dev[:, tensor_slot], axis=0)))
            grad_bkv = grad_bkv.at[value_col:value_col + HD].add(lax.optimization_barrier(jnp.sum(grad_value_dev[:, tensor_slot], axis=0)))
        back_one, gain_one = norm_backward(grad_act_one, normed_one, scale_one, gain_attn)
        grad_rows = (grad_hidden + back_one).astype(jnp.bfloat16)
        new_totals = (totals[0] + gain_one, totals[1] + matmul(act_one.T, grad_query_low), totals[2] + lax.optimization_barrier(jnp.sum(grad_query, axis=0)), totals[3] + grad_wkv, totals[4] + grad_bkv, totals[5] + matmul(context.T, grad_attn), totals[6] + gain_two, totals[7] + matmul(act_two.T, grad_gate), totals[8] + matmul(act_two.T, grad_up), totals[9] + matmul(mixed_rows.T, rows_cot))
        return (new_totals, (block_out, grad_rows))
    init_totals = (jnp.zeros((D,), jnp.float32), jnp.zeros((D, HQ * HD), jnp.float32), jnp.zeros((HQ * HD,), jnp.float32), jnp.zeros((D, 2 * KV * HD), jnp.float32), jnp.zeros((2 * KV * HD,), jnp.float32), jnp.zeros((HQ * HD, D), jnp.float32), jnp.zeros((D,), jnp.float32), jnp.zeros((D, FF), jnp.float32), jnp.zeros((D, FF), jnp.float32), jnp.zeros((FF, D), jnp.float32))
    totals, (outputs, grads) = lax.scan(one_sequence, init_totals, (inputs_seq, segment_ids, cot_seq))
    return (outputs.reshape(seq_count * seq_length, D), grads.reshape(seq_count * seq_length, D), totals[0], totals[1], totals[2], totals[3], totals[4], totals[5], totals[6], totals[7], totals[8], totals[9])
```

```python
import math

import jax
import jax.numpy as jnp
from jax import lax
from jax.sharding import PartitionSpec as P

HQ = 12
KV = 2
HD = 128

epsilon = 1e-06
rope_base = 1000000.0
masked_score = -1e30


bf16 = jnp.bfloat16
f32 = jnp.float32


def dot(left, right, dims):
    return lax.dot_general(left, right, (dims, ((), ())), preferred_element_type=f32)


def nn(left, right):
    return dot(left, right, ((1,), (0,)))


def nt(left, right):
    return dot(left, right, ((1,), (1,)))


def tn(left, right):
    return dot(left, right, ((0,), (0,)))


def positions_of(segment_row):
    index_row = jnp.arange(segment_row.shape[0], dtype=jnp.int32)
    starts = jnp.concatenate(
        [jnp.ones((1,), jnp.int32), (segment_row[1:] != segment_row[:-1]).astype(jnp.int32)]
    )
    first_index = lax.cummax(jnp.where(starts > 0, index_row, 0), axis=0)
    return index_row - first_index


def rotary(positions):
    inverse = rope_base ** (-(jnp.arange(HD // 2, dtype=f32) * 2.0 / HD))
    angles = positions.astype(f32)[:, None] * inverse[None, :]
    cosine, sine = jnp.cos(angles), jnp.sin(angles)
    return (
        jnp.concatenate([cosine, cosine], axis=1),
        jnp.concatenate([sine, sine], axis=1),
    )


def turn(values_in, cosine_table, sine_table):
    half_size = values_in.shape[-1] // 2
    rolled = jnp.concatenate([-values_in[..., half_size:], values_in[..., :half_size]], axis=-1)
    return values_in * cosine_table + rolled * sine_table


def norm_forward(values_in):
    row_scale = lax.rsqrt(jnp.mean(values_in * values_in, axis=-1, keepdims=True) + epsilon)
    return (values_in * row_scale, row_scale)


def norm_backward(grad_out, normed, row_scale, gain_vec):
    grad_normed = grad_out * gain_vec
    grad_in = row_scale * (
        grad_normed - normed * jnp.mean(grad_normed * normed, axis=-1, keepdims=True)
    )
    return (grad_in, jnp.sum(grad_out * normed, axis=0))


class Links:
    def __init__(self, n_dp, n_tensor):
        self.n_dp, self.n_tensor = n_dp, n_tensor
        self.pair = 2
        self.group_bits = [1 << k for k in reversed(range(n_dp.bit_length() - 1)) if 1 << k != 2]
        self.all_bits = [2] + self.group_bits

    def dp(self, value, bit):
        return lax.ppermute(value, "dp", [(i, i ^ bit) for i in range(self.n_dp)])

    def tensor(self, value, bit):
        return lax.ppermute(value, "tensor", [(i, i ^ bit) for i in range(self.n_tensor)])

    def gather(self, pieces, bits):
        for bit in bits:
            pieces = {**pieces, **{key ^ bit: self.dp(val, bit) for key, val in pieces.items()}}
        return pieces

    def reduce_bits(self, blocks, bits, index):
        widths = [1 << k for k in reversed(range(self.n_dp.bit_length() - 1))]
        shape = blocks.shape[1:]
        held = blocks.reshape((2,) * len(widths) + shape)
        left = list(widths)
        for bit in bits:
            axis = left.index(bit)
            mine = ((index // bit) % 2).astype(jnp.int32)
            send = lax.dynamic_index_in_dim(held, 1 - mine, axis, keepdims=False)
            keep = lax.dynamic_index_in_dim(held, mine, axis, keepdims=False)
            got = self.dp(send, bit)
            held = (keep.astype(f32) + got.astype(f32)).astype(bf16)
            left.pop(axis)
        return held

    def gather_rows(self, own):
        half = jnp.concatenate([own, self.tensor(own, 2)], axis=0)
        return jnp.concatenate([half, self.tensor(half, 1)], axis=0)

    def reduce_rows(self, matmul_rows, count):
        got = self.tensor(matmul_rows(2 * count, 4 * count).astype(bf16), 1)
        held = matmul_rows(0, 2 * count) + got.astype(f32)
        got = self.tensor(held[count:].astype(bf16), 2)
        return held[:count] + got.astype(f32)

    def gather_pair(self, own):
        half = own.shape[0] // 2
        from_x = self.tensor(own, 2)
        from_z = self.dp(own, self.pair)
        corner_a = self.dp(from_x[:half], self.pair)
        corner_b = self.tensor(from_z[half:], 2)
        four = jnp.concatenate([own, from_x, from_z, corner_a, corner_b], axis=0)
        return jnp.concatenate([four, self.tensor(four, 1)], axis=0)

    def reduce_pair(self, matmul_rows, count):
        half = count // 2
        got = self.tensor(matmul_rows(4 * count, 8 * count).astype(bf16), 1)
        held = matmul_rows(0, 4 * count) + got.astype(f32)
        own, of_x, of_z, of_xz = (held[k * count : (k + 1) * count] for k in range(4))
        send_a = jnp.concatenate([of_x[:half], of_xz[:half]], axis=0).astype(bf16)
        send_b = jnp.concatenate([of_z[half:], of_xz[half:]], axis=0).astype(bf16)
        got_a = self.tensor(send_a, 2).astype(f32)
        got_b = self.dp(send_b, self.pair).astype(f32)
        last_a = self.dp((of_z[:half] + got_a[half:]).astype(bf16), self.pair)
        last_b = self.tensor((of_x[half:] + got_b[half:]).astype(bf16), 2)
        return jnp.concatenate(
            [
                own[:half] + got_a[:half] + last_a.astype(f32),
                own[half:] + got_b[:half] + last_b.astype(f32),
            ],
            axis=0,
        )


def assemble(pieces, index, n_dp):
    rows, cols = pieces[0].shape
    whole = jnp.zeros((n_dp * rows, cols), pieces[0].dtype)
    for key, val in pieces.items():
        whole = lax.dynamic_update_slice_in_dim(whole, val, (index ^ key) * rows, 0)
    return whole


def local_of(n_dp, n_tensor):
    links = Links(n_dp, n_tensor)

    def local(
        block_input,
        segment_ids,
        gain_attn,
        w_query,
        b_query,
        w_keyval,
        b_keyval,
        w_out,
        gain_ffn,
        w_gate,
        w_up,
        w_down,
        cotangent,
    ):
        dp_index = lax.axis_index("dp")
        tensor_index = lax.axis_index("tensor")
        count, width = block_input.shape
        row_count = count * n_tensor
        local_heads = b_query.shape[0] // HD
        q_cols = local_heads * HD
        head_kv = tensor_index * local_heads // (HQ // KV)
        wide_rows = width // n_dp
        units = w_gate.shape[1]
        half_units = -(-units // 256) * 128
        pair_side = (dp_index // 2) % 2

        rows_float = block_input.astype(f32)
        normed_one, scale_one = norm_forward(rows_float)
        act_one = links.gather_rows((normed_one * gain_attn).astype(bf16))

        own_key_w = lax.dynamic_slice_in_dim(w_keyval, head_kv * HD, HD, 1)
        own_value_w = lax.dynamic_slice_in_dim(w_keyval, (KV + head_kv) * HD, HD, 1)
        attn_slot = jnp.concatenate([w_query, own_key_w, own_value_w, w_out.T], axis=1)
        attn_w = assemble(links.gather({0: attn_slot}, links.all_bits), dp_index, n_dp)
        qkv_w = attn_w[:, : q_cols + 2 * HD]
        out_w = attn_w[:, q_cols + 2 * HD :]

        def ffn_weight(weight):
            padded = jnp.pad(weight, ((0, 0), (0, 2 * half_units - units)))
            mine = lax.dynamic_slice_in_dim(padded, pair_side * half_units, half_units, 1)
            other = lax.dynamic_slice_in_dim(padded, (1 - pair_side) * half_units, half_units, 1)
            both = jnp.concatenate([mine, links.dp(other, links.pair)], axis=0)
            pieces = links.gather({0: both}, links.group_bits)
            split = {}
            for key, val in pieces.items():
                split[key] = val[:wide_rows]
                split[key ^ links.pair] = val[wide_rows:]
            return assemble(split, dp_index, n_dp)

        gate_w = ffn_weight(w_gate)
        up_w = ffn_weight(w_up)
        down_w = ffn_weight(w_down.T)
        cot_pair = links.gather_pair(cotangent)

        blocks = jnp.stack([tensor_index ^ k for k in (0, 2, 1, 3)])
        token_index = (blocks[:, None] * count + jnp.arange(count)[None, :]).reshape(row_count)
        positions_row = positions_of(segment_ids[0]).reshape(n_tensor, count)
        segment_row = segment_ids[0].reshape(n_tensor, count)
        pick = lambda table: jnp.concatenate(
            [lax.dynamic_index_in_dim(table, tensor_index ^ k, 0, keepdims=False) for k in (0, 2, 1, 3)]
        )
        positions = pick(positions_row)
        segments = pick(segment_row)
        cosine_table, sine_table = rotary(positions)
        cos_heads, sin_heads = cosine_table[:, None, :], sine_table[:, None, :]
        allowed = (token_index[:, None] >= token_index[None, :]) & (
            segments[:, None] == segments[None, :]
        )

        qkv = nn(act_one, qkv_w)
        query_rows = qkv[:, :q_cols] + b_query
        key_rows = qkv[:, q_cols : q_cols + HD] + lax.dynamic_slice_in_dim(
            b_keyval, head_kv * HD, HD, 0
        )
        value_rows = (
            qkv[:, q_cols + HD :] + lax.dynamic_slice_in_dim(b_keyval, (KV + head_kv) * HD, HD, 0)
        ).astype(bf16)
        query_rot = turn(
            query_rows.reshape(row_count, local_heads, HD), cos_heads, sin_heads
        ).astype(bf16)
        key_rot = turn(key_rows, cosine_table, sine_table).astype(bf16)

        def masked_scores():
            raw_scores = jnp.einsum(
                "qhd,kd->hqk", query_rot, key_rot, preferred_element_type=f32
            ) / math.sqrt(HD)
            return jnp.where(allowed[None], raw_scores, masked_score)

        scores = masked_scores()
        row_max = jnp.max(scores, axis=2, keepdims=True)
        log_total = row_max + jnp.log(jnp.sum(jnp.exp(scores - row_max), axis=2, keepdims=True))
        probs_low = jnp.exp(scores - log_total).astype(bf16)
        attn_result = jnp.einsum("hqk,kd->qhd", probs_low, value_rows, preferred_element_type=f32)
        context = attn_result.astype(bf16).reshape(row_count, q_cols)

        hidden = rows_float + links.reduce_rows(lambda lo, hi: nt(context[lo:hi], out_w), count)
        normed_two, scale_two = norm_forward(hidden)
        act_two = links.gather_pair((normed_two * gain_ffn).astype(bf16))

        gate_pre = nn(act_two, gate_w)
        up_part = nn(act_two, up_w)
        grad_mixed = nn(cot_pair, down_w)
        sigmoid_gate = jax.nn.sigmoid(gate_pre)
        silu_gate = gate_pre * sigmoid_gate
        mixed_rows = (silu_gate * up_part).astype(bf16)
        grad_gate = (
            grad_mixed * up_part * sigmoid_gate * (1.0 + gate_pre * (1.0 - sigmoid_gate))
        ).astype(bf16)
        grad_up = (grad_mixed * silu_gate).astype(bf16)
        grad_act_two = links.reduce_pair(
            lambda lo, hi: nt(grad_gate[lo:hi], gate_w) + nt(grad_up[lo:hi], up_w), count
        )
        back_two, gain_two = norm_backward(grad_act_two, normed_two, scale_two, gain_ffn)
        grad_hidden = cotangent.astype(f32) + back_two
        grad_attn = links.gather_rows(grad_hidden.astype(bf16))

        def ffn_grad(left, right):
            blocks = tn(left, right).astype(bf16).reshape(n_dp, wide_rows, half_units)
            held = links.reduce_bits(blocks, list(reversed(links.group_bits)), dp_index)
            send = lax.dynamic_index_in_dim(held, 1 - pair_side, 0, keepdims=False)
            mine = lax.dynamic_index_in_dim(held, pair_side, 0, keepdims=False)
            other = links.dp(send, links.pair)
            first = jnp.where(pair_side == 0, mine, other)
            second = jnp.where(pair_side == 0, other, mine)
            return jnp.concatenate([first, second[:, : units - half_units]], axis=1).astype(f32)

        down_share = ffn_grad(cot_pair, mixed_rows).T
        gate_share = ffn_grad(act_two, grad_gate)
        up_share = ffn_grad(act_two, grad_up)
        block_out = (
            hidden + links.reduce_pair(lambda lo, hi: nt(mixed_rows[lo:hi], down_w), count)
        ).astype(bf16)

        def attn_grad(left, right):
            blocks = tn(left, right).astype(bf16).reshape(n_dp, wide_rows, right.shape[1])
            return links.reduce_bits(blocks, list(reversed(links.group_bits)) + [2], dp_index)

        out_share = attn_grad(grad_attn, context).astype(f32).T
        grad_context = nt_context = nn(grad_attn, out_w).astype(bf16)
        grad_context = nt_context.reshape(row_count, local_heads, HD)
        scores = masked_scores()
        attn_probs = jnp.exp(scores - log_total)
        probs_low = attn_probs.astype(bf16)
        grad_probs = jnp.einsum(
            "qhd,kd->hqk", grad_context, value_rows, preferred_element_type=f32
        )
        row_delta = jnp.sum(grad_context.astype(f32) * attn_result, axis=2).T[:, :, None]
        grad_scores = (attn_probs * (grad_probs - row_delta)).astype(bf16)
        grad_query_rot = jnp.einsum(
            "hqk,kd->qhd", grad_scores, key_rot, preferred_element_type=f32
        ) / math.sqrt(HD)
        grad_key_rot = jnp.einsum(
            "hqk,qhd->kd", grad_scores, query_rot, preferred_element_type=f32
        ) / math.sqrt(HD)
        grad_value = jnp.einsum("hqk,qhd->kd", probs_low, grad_context, preferred_element_type=f32)
        grad_query = turn(grad_query_rot, cos_heads, -sin_heads).reshape(row_count, q_cols)
        grad_key = turn(grad_key_rot, cosine_table, -sine_table)
        grad_low = jnp.concatenate(
            [grad_query.astype(bf16), grad_key.astype(bf16), grad_value.astype(bf16)], axis=1
        )
        grad_act_one = links.reduce_rows(lambda lo, hi: nt(grad_low[lo:hi], qkv_w), count)
        back_one, gain_one = norm_backward(grad_act_one, normed_one, scale_one, gain_attn)
        grad_rows = (grad_hidden + back_one).astype(bf16)

        qkv_share = attn_grad(act_one, grad_low)
        query_share = qkv_share[:, :q_cols].astype(f32)
        side_c, side_x = tensor_index % 2, tensor_index // 2
        kv_blocks = qkv_share[:, q_cols:].reshape(2, 2, wide_rows // 4, 2 * HD)
        kv_got = links.tensor(lax.dynamic_index_in_dim(kv_blocks, 1 - side_c, 1, keepdims=False), 1)
        kv_held = (
            lax.dynamic_index_in_dim(kv_blocks, side_c, 1, keepdims=False).astype(f32)
            + kv_got.astype(f32)
        )
        kv_mine = lax.dynamic_index_in_dim(kv_held, side_x, 0, keepdims=False)
        kv_other = links.tensor(lax.dynamic_index_in_dim(kv_held, 1 - side_x, 0, keepdims=False), 2)
        kv_first = jnp.where(side_x == 0, kv_mine, kv_other)
        kv_second = jnp.where(side_x == 0, kv_other, kv_mine)
        keyval_share = jnp.concatenate(
            [kv_first[:, :HD], kv_second[:, :HD], kv_first[:, HD:], kv_second[:, HD:]], axis=1
        )

        n_all = n_dp * n_tensor
        bias_query = lax.dynamic_update_slice_in_dim(
            jnp.zeros((HQ * HD,), f32), jnp.sum(grad_query, axis=0), tensor_index * q_cols, 0
        )
        bias_keyval = lax.dynamic_update_slice_in_dim(
            jnp.zeros((2 * KV * HD,), f32), jnp.sum(grad_key, axis=0), head_kv * HD, 0
        )
        bias_keyval = lax.dynamic_update_slice_in_dim(
            bias_keyval, jnp.sum(grad_value, axis=0), (KV + head_kv) * HD, 0
        )
        small = [gain_one, gain_two, bias_query, bias_keyval]
        packed = jnp.concatenate([val.reshape(n_all, -1) for val in small], axis=1)
        sizes = [val.shape[0] // n_all for val in small]
        summed = lax.psum_scatter(
            packed.reshape(-1), ("dp", "tensor"), scatter_dimension=0, tiled=True
        )
        ends = [sum(sizes[: k + 1]) for k in range(4)]
        gain_one_share, gain_two_share, query_bias_share, keyval_bias_share = (
            summed[end - size : end] for end, size in zip(ends, sizes)
        )
        return (
            block_out,
            grad_rows,
            gain_one_share,
            query_share,
            query_bias_share,
            keyval_share,
            keyval_bias_share,
            out_share,
            gain_two_share,
            gate_share,
            up_share,
            down_share,
        )

    return local


def solution(mesh):
    placed = (
        P(("dp", "tensor"), None),
        P("dp", None),
        P(),
        P("dp", "tensor"),
        P("tensor"),
        P("dp", None),
        P(),
        P("tensor", "dp"),
        P(),
        P("dp", "tensor"),
        P("dp", "tensor"),
        P("tensor", "dp"),
        P(("dp", "tensor"), None),
    )
    return jax.shard_map(
        local_of(mesh.shape["dp"], mesh.shape["tensor"]),
        mesh=mesh,
        in_specs=placed,
        out_specs=(
            P(("dp", "tensor"), None),
            P(("dp", "tensor"), None),
            P(("dp", "tensor")),
            P("dp", "tensor"),
            P(("dp", "tensor")),
            P(("dp", "tensor"), None),
            P(("dp", "tensor")),
            P("tensor", "dp"),
            P(("dp", "tensor")),
            P("dp", "tensor"),
            P("dp", "tensor"),
            P("tensor", "dp"),
        ),
        check_vma=False,
    )
```
